768 devices in a mesh: dp: 48 (over x, z), pipe: 8 (over y_lo, core), mp: 2 (over y_hi).
Axes of the slice: x: 4, y: 8 (y_hi: 2, y_lo: 4; y = y_hi * 4 + y_lo), z: 12, core: 2. Of those that a mesh axis runs over, the one named last changes fastest.
Arguments:
- latents: bfloat16 [48, 2, 64, 3072], P('dp'), may hold values from -6 to 6
- caption_kv: bfloat16 [48, 8, 2, 128, 1536], P('dp', 'pipe', None, None, 'mp'), may hold values from -6 to 6
- caption_mask: int32 [48, 128], P('dp'), may hold values from 0 to 1, as said below
- query_weight: bfloat16 [8, 3072, 1536], P('pipe', None, 'mp'), may hold values from -0.109375 to 0.109375
- out_weight: bfloat16 [8, 1536, 3072], P('pipe', 'mp'), may hold values from -0.15625 to 0.15625
- gate: float32 [8, 3072], P('pipe'), may hold values from 0.5 to 1.5
- cotangent: bfloat16 [48, 2, 64, 3072], P('dp'), may hold values from -6 to 6
Outputs:
- section_out: bfloat16 [8, 48, 2, 64, 3072], P('pipe', 'dp', None, None, 'mp')
- input_grad: bfloat16 [8, 48, 2, 64, 3072], P('pipe', 'dp', None, None, 'mp')
- out_weight_grad: float32 [8, 1536, 3072], P('pipe', 'mp', 'dp')
The draws below stay inside these ranges and needn't reach their ends.
Inputs may be any that keep to these rules, and one draw needn't show every extreme that they name: `caption_mask`: each row is a run of ones followed by zeros; the first 32 entries of every row are 1, and some row is all ones.
All inputs are finite; a program needn't handle non-finite values.
Results may differ from the reference program's by a relative error of at most 0.04.
Values may be sent and summed in bfloat16 or wider, within the bound.
No kernel may reach another device: no remote copies, remote signals or barrier semaphores. Data moves between devices by JAX's collectives and lax.ppermute only.
A program may use at most 64 MiB of HBM per device.

```python
import math
from functools import partial
import jax
import jax.numpy as jnp
from jax import lax

D = 3072
HEADS = 12
HEAD_DIM = 128
CAP = 128
TOK = 64
MICRO = 2
N_DP = 48
N_PIPE = 8


def draw_caption_mask(key, part):
    lengths = jax.random.randint(key, (N_DP,), CAP // 4, CAP + 1)
    lengths = lengths.at[0].set(CAP)
    positions = jnp.arange(CAP, dtype=jnp.int32)
    return (positions[None, :] < lengths[:, None]).astype(jnp.int32)


def with_spikes(drawn, key, source, target, parts, factor):
    owner, partner = [(jnp.arange(drawn.shape[dim]) // (drawn.shape[dim] // parts)).reshape([-1 if axis == dim else 1 for axis in range(drawn.ndim)]) for dim in (source, target)]
    chosen = jax.random.permutation(key, parts)[partner]
    strong = (owner == chosen) | (owner == (partner + parts // 2) % parts)
    return jnp.where(strong, factor * drawn, drawn)


def block_levels(own_key, shape, pieces, smallest, high):
    level = 1.0
    for dim, parts in pieces:
        draws = jax.random.uniform(jax.random.fold_in(jax.random.fold_in(own_key, 6), dim), (parts,), jnp.float32, smallest / len(pieces), high / len(pieces))
        level = level * jnp.repeat(jnp.exp(draws), shape[dim] // parts).reshape((-1,) + (1,) * (len(shape) - 1 - dim))
    return level


def bell_draw(stream_key, extent, deviation, reach, cuts=(), held_as=jnp.bfloat16):
    array = jax.random.normal(stream_key, extent, jnp.float32) * deviation
    if len(cuts) > 0:
        array = block_levels(stream_key, extent, cuts, -0.22, 0.18) * array
    return jnp.clip(array, min=-reach, max=reach).astype(held_as)


def bell_draw_with(rng, extent, spread, bound, cuts, heavy, kind=jnp.bfloat16):
    array = spread * jax.random.normal(rng, extent, jnp.float32)
    if cuts:
        array = array * block_levels(rng, extent, cuts, -0.22, 0.18)
    return jnp.clip(with_spikes(array, jax.random.fold_in(rng, 3), *heavy), -bound, bound).astype(kind)


def setup_inputs(seed: int = 0) -> dict:
    splits = jax.random.split(jax.random.key(seed), 8)
    return {
        "latents": bell_draw(splits[0], (N_DP, MICRO, TOK, D), 1.0, 6.0, ((0, 48),)),
        "caption_kv": bell_draw(splits[1], (N_DP, N_PIPE, 2, CAP, HEADS * HEAD_DIM), 1.0, 6.0, ((0, 48), (1, 8), (4, 2))),
        "caption_mask": draw_caption_mask(jax.random.fold_in(splits[7], 71), 0),
        "query_weight": bell_draw(splits[3], (N_PIPE, D, HEADS * HEAD_DIM), D ** -0.5, 0.109375, ((0, 8), (2, 2))),
        "out_weight": bell_draw(splits[4], (N_PIPE, HEADS * HEAD_DIM, D), (HEADS * HEAD_DIM) ** -0.5, 0.15625, ((0, 8), (1, 2))),
        "gate": jnp.clip(0.5 + 1.0 * jax.random.uniform(splits[5], (N_PIPE, D), jnp.float32) ** block_levels(splits[5], (N_PIPE, D), ((0, 8),), -0.2, 0.2), 0.5, 1.5),
        "cotangent": bell_draw_with(splits[6], (N_DP, MICRO, TOK, D), 1.0, 6.0, ((0, 48),), (0, 3, 48, 3.25)),
    }


def forward_parts(x_rows, w_query, kv_pair, live):
    rows = x_rows.shape[0]
    x_float = x_rows.astype(jnp.float32)
    scale_r = lax.rsqrt(lax.optimization_barrier(jnp.mean(x_float * x_float, axis=-1, keepdims=True)) + 1e-06)
    normed = (x_float * scale_r).astype(jnp.bfloat16)
    query = jnp.dot(normed, w_query, preferred_element_type=jnp.float32).astype(jnp.bfloat16)
    q_heads = query.reshape(rows, -1, HEAD_DIM).astype(jnp.float32)
    k_heads = kv_pair[0].reshape(kv_pair.shape[1], -1, HEAD_DIM).astype(jnp.float32)
    v_heads = kv_pair[1].reshape(kv_pair.shape[1], -1, HEAD_DIM).astype(jnp.float32)
    scores = jnp.einsum('rhd,chd->hrc', q_heads, k_heads) / math.sqrt(HEAD_DIM)
    scores = jnp.where(live[None, None, :] > 0, scores, -1e+30)
    prob = jax.nn.softmax(scores, axis=-1)
    probs = lax.optimization_barrier(prob.astype(jnp.bfloat16)).astype(jnp.float32)
    attended = jnp.einsum('hrc,chd->rhd', probs, v_heads).reshape(rows, -1).astype(jnp.bfloat16)
    return (x_float, scale_r, prob, attended, k_heads, v_heads)

def section_forward(x_rows, w_query, w_out, kv_pair, live, gain):
    x_float, scale_r, prob, attended, k_heads, v_heads = forward_parts(x_rows, w_query, kv_pair, live)
    proj = jnp.dot(attended, w_out, preferred_element_type=jnp.float32)
    return (x_float + gain * proj).astype(jnp.bfloat16)

def section_backward(x_rows, grad_rows, w_query, w_out, kv_pair, live, gain):
    rows = x_rows.shape[0]
    x_float, scale_r, prob, attended, k_heads, v_heads = forward_parts(x_rows, w_query, kv_pair, live)
    grad_float = grad_rows.astype(jnp.float32)
    dproj = (gain * grad_float).astype(jnp.bfloat16)
    dattended = jnp.dot(dproj, w_out.T, preferred_element_type=jnp.float32).astype(jnp.bfloat16)
    d_heads = dattended.reshape(rows, -1, HEAD_DIM).astype(jnp.float32)
    dprob = jnp.einsum('rhd,chd->hrc', d_heads, v_heads)
    dscore = (prob * (dprob - lax.optimization_barrier(jnp.sum(prob * dprob, axis=-1, keepdims=True)))).astype(jnp.bfloat16)
    dscore_f = lax.optimization_barrier(dscore).astype(jnp.float32)
    dquery = (jnp.einsum('hrc,chd->rhd', dscore_f, k_heads) / math.sqrt(HEAD_DIM)).reshape(rows, -1).astype(jnp.bfloat16)
    dnormed = jnp.dot(dquery, w_query.T, preferred_element_type=jnp.float32)
    inner = lax.optimization_barrier(jnp.mean(dnormed * x_float, axis=-1, keepdims=True))
    dx = (grad_float + scale_r * (dnormed - x_float * (scale_r * scale_r) * inner)).astype(jnp.bfloat16)
    return (dx, attended, dproj)

def reference(latents, caption_kv, caption_mask, query_weight, out_weight, gate, cotangent):
    samples, micro, tok, width = latents.shape
    current = latents.reshape(samples, micro * tok, width)
    inputs = []
    outputs = []
    for section in range(N_PIPE):
        step_fn = jax.vmap(partial(section_forward, w_query=query_weight[section], w_out=out_weight[section], gain=gate[section]))
        result = step_fn(current, kv_pair=caption_kv[:, section], live=caption_mask)
        inputs.append(current)
        outputs.append(result)
        current = result
    upstream = cotangent.reshape(samples, micro * tok, width)
    grads = [None] * N_PIPE
    weight_grads = [None] * N_PIPE
    for section in range(N_PIPE - 1, -1, -1):
        back_fn = jax.vmap(partial(section_backward, w_query=query_weight[section], w_out=out_weight[section], gain=gate[section]))
        dx, attended, dproj = back_fn(inputs[section], upstream, kv_pair=caption_kv[:, section], live=caption_mask)
        weight_grads[section] = jnp.einsum('srk,srd->kd', attended.astype(jnp.float32), dproj.astype(jnp.float32))
        grads[section] = dx
        upstream = dx
    section_out = jnp.stack(outputs).reshape(N_PIPE, samples, micro, tok, width)
    input_grad = jnp.stack(grads).reshape(N_PIPE, samples, micro, tok, width)
    return (section_out, input_grad, jnp.stack(weight_grads))
```

```python
import math
from functools import partial

import jax
import jax.numpy as jnp
from jax import lax
from jax.experimental import pallas as pl
from jax.experimental.pallas import tpu as pltpu
from jax.sharding import PartitionSpec as P

HEAD_DIM = 128
CHUNKS = 2
EPS = 1e-06
TILE = 1024
TILE_BACK = 1024
NARROW = 256
SPLIT = 2
FILL = 128
BF16 = jnp.bfloat16
F32 = jnp.float32


def nt(a, b):
    return lax.dot_general(a, b, (((1,), (1,)), ((), ())), preferred_element_type=F32)


def nn(a, b):
    rows = a.shape[0]
    if rows < FILL:
        a = jnp.concatenate([a] * (FILL // rows), axis=0)
    return jnp.dot(a, b, preferred_element_type=F32)[:rows]


def head_cols(inner):
    return [slice(h * HEAD_DIM, (h + 1) * HEAD_DIM) for h in range(inner // HEAD_DIM)]


def load_kernel(wq_in, wo_in, kv_in, mask_in, gate_in, wq, wo, kv, mask, gate, *rest):
    sems = rest[-1]
    pairs = [(wq_in, wq), (kv_in, kv), (mask_in, mask), (gate_in, gate), (wo_in, wo)]
    moves = [pltpu.make_async_copy(src, dst, sems.at[i]) for i, (src, dst) in enumerate(pairs)]
    for move in moves:
        move.start()
    for move in moves:
        move.wait()


def fetch(a, b, edge_in, av, bv, edge, chunk, sems):
    near = pltpu.make_async_copy(a, av, sems.at[0])
    far = pltpu.make_async_copy(b, bv, sems.at[1])
    own = pltpu.make_async_copy(edge_in.at[chunk], av, sems.at[0])

    @pl.when(~edge)
    def _():
        near.start()
        far.start()
        near.wait()
        far.wait()

    @pl.when(edge)
    def _():
        own.start()
        bv[...] = jnp.zeros_like(bv)
        own.wait()


def half_copies(values, share, side, chunk, own, other, sems):
    moves = []
    for which in range(2):
        mine = pl.ds(which * share, share)
        rest = pl.ds((1 - which) * share, share)
        group = [pltpu.make_async_copy(values.at[:, mine], own.at[chunk], sems.at[0])]
        if other is not None:
            group.append(pltpu.make_async_copy(values.at[:, rest], other.at[chunk], sems.at[1]))
        moves.append((side == which, group))
    return moves


def start_moves(moves):
    for wanted, group in moves:

        @pl.when(wanted)
        def _():
            for move in group:
                move.start()


def wait_moves(moves):
    for wanted, group in moves:

        @pl.when(wanted)
        def _():
            for move in group:
                move.wait()


def forward_kernel(step, sections, info, a, b, first_in, wq, wo, kv, mask, gate, *rest):
    out, xs, qr, pr, at, xh, own, other, av, bv, atv, outv, sems = rest[7:]
    rows, width = av.shape
    inner = wo.shape[0]
    share = width // 2
    heads = head_cols(inner)
    place, side = info[0], info[1]
    chunk = step - place

    @pl.when((chunk >= 0) & (chunk < CHUNKS))
    def _():
        fetch(a, b, first_in, av, bv, place == 0, chunk, sems)
        x = (av[...].astype(F32) + bv[...].astype(F32)).astype(BF16)
        xs[chunk] = x
        save_x = half_copies(xs.at[chunk], share, side, chunk, xh, None, sems.at[pl.ds(3, 2)])
        start_moves(save_x)
        xf = x.astype(F32)
        scale = lax.rsqrt(jnp.sum(xf * xf, axis=1, keepdims=True) / width + EPS)
        split = width // SPLIT

        @pl.loop(0, SPLIT)
        def _(i):
            deep = pl.ds(pl.multiple_of(i * split, split), split)
            value = nn(xs[chunk, :, deep], wq[deep, :])

            @pl.when(i == 0)
            def _():
                qr[chunk] = value

            @pl.when(i > 0)
            def _():
                qr[chunk] += value

        query = (qr[chunk] * scale).astype(BF16)
        live = mask[...] > 0
        ss = [nt(query[:, c], kv[0, :, c]) for c in heads]
        ss = [jnp.where(live, s * (1 / math.sqrt(HEAD_DIM)), -1e30) for s in ss]
        es = [jnp.exp(s - jnp.max(s, axis=1, keepdims=True)) for s in ss]
        ps = [e * (1 / jnp.sum(e, axis=1, keepdims=True)) for e in es]
        os = [nn(p.astype(BF16), kv[1, :, c]).astype(BF16) for p, c in zip(ps, heads)]
        for p, o, c in zip(ps, os, heads):
            pr[chunk, :, c] = p
            atv[:, c] = o
        save_a = pltpu.make_async_copy(atv, at.at[chunk], sems.at[5])
        save_a.start()
        lead = (1 - side).astype(F32)

        @pl.loop(0, width // TILE)
        def _(i):
            cols = pl.ds(pl.multiple_of(i * TILE, TILE), TILE)
            proj = nn(atv[...], wo[:, cols])
            outv[:, cols] = (lead * xs[chunk, :, cols].astype(F32) + gate[:, cols] * proj).astype(BF16)

        send = pltpu.make_async_copy(outv, out, sems.at[2])
        send.start()
        if step >= sections - 1:
            final = half_copies(outv, share, side, chunk, own, other, sems.at[pl.ds(6, 2)])

            @pl.when(place == sections - 1)
            def _():
                start_moves(final)
                wait_moves(final)

        save_a.wait()
        wait_moves(save_x)
        send.wait()


def backward_kernel(step, sections, info, a, b, last_in, wq, wo, kv, gate, *rest):
    out, xs, qr, pr, dp, dyh, own, other, av, bv, dpv, dav, dqv, outv, sems = rest[7:]
    rows, width = av.shape
    inner = wo.shape[0]
    share = width // 2
    heads = head_cols(inner)
    place, side = info[0], info[1]
    chunk = step - (sections - 1 - place)

    @pl.when((chunk >= 0) & (chunk < CHUNKS))
    def _():
        fetch(a, b, last_in, av, bv, place == sections - 1, chunk, sems)
        grad = (av[...].astype(F32) + bv[...].astype(F32)).astype(BF16)
        av[...] = grad
        dpv[...] = (gate[...] * grad.astype(F32)).astype(BF16)
        save_p = pltpu.make_async_copy(dpv, dp.at[chunk], sems.at[5])
        save_p.start()
        save_y = half_copies(av, share, side, chunk, dyh, None, sems.at[pl.ds(3, 2)])
        start_moves(save_y)

        @pl.loop(0, inner // NARROW)
        def _(i):
            cols = pl.ds(pl.multiple_of(i * NARROW, NARROW), NARROW)
            dav[:, cols] = nt(dpv[...], wo[cols, :]).astype(BF16)

        dprobs = [nt(dav[:, c], kv[1, :, c]) for c in heads]
        ps = [pr[chunk, :, c] for c in heads]
        rs = [jnp.sum(p * d, axis=1, keepdims=True) for p, d in zip(ps, dprobs)]
        ds = [(p * (d - r)).astype(BF16) for p, d, r in zip(ps, dprobs, rs)]
        dqs = [(nn(d, kv[0, :, c]) * (1 / math.sqrt(HEAD_DIM))).astype(BF16) for d, c in zip(ds, heads)]
        total = jnp.zeros((rows, HEAD_DIM), F32)
        for dq, c in zip(dqs, heads):
            dqv[:, c] = dq
            total = total + dq.astype(F32) * qr[chunk, :, c]
        mean = jnp.sum(total, axis=1, keepdims=True) / width
        xf = xs[chunk].astype(F32)
        scale = lax.rsqrt(jnp.sum(xf * xf, axis=1, keepdims=True) / width + EPS)
        coeff = scale * scale * mean
        lead = (1 - side).astype(F32)

        @pl.loop(0, width // TILE_BACK)
        def _(i):
            cols = pl.ds(pl.multiple_of(i * TILE_BACK, TILE_BACK), TILE_BACK)
            dn = nt(dqv[...], wq[cols, :])
            piece = scale * (dn - xs[chunk, :, cols].astype(F32) * coeff)
            outv[:, cols] = (lead * av[:, cols].astype(F32) + piece).astype(BF16)

        send = pltpu.make_async_copy(outv, out, sems.at[2])
        send.start()
        if step >= sections - 1:
            final = half_copies(outv, share, side, chunk, own, other, sems.at[pl.ds(6, 2)])

            @pl.when(place == 0)
            def _():
                start_moves(final)
                wait_moves(final)

        save_p.wait()
        wait_moves(save_y)
        send.wait()


ANY = pl.BlockSpec(memory_space=pl.ANY)
SMEM = pl.BlockSpec(memory_space=pltpu.SMEM)
VMEM = pl.BlockSpec(memory_space=pltpu.VMEM)
LIMIT = 16 << 20


def held(x):
    return pltpu.VMEM(x.shape, x.dtype)


def run_load(fixed, typed, free):
    return pl.pallas_call(
        load_kernel,
        out_shape=(*map(held, fixed), *typed, *free),
        in_specs=[ANY] * 5,
        out_specs=(VMEM,) * (5 + len(typed)) + (ANY,) * len(free),
        scratch_shapes=[pltpu.SemaphoreType.DMA((5,))],
        compiler_params=pltpu.CompilerParams(vmem_limit_bytes=LIMIT),
        name="load_weights",
    )(*fixed)


def run_step(kernel, name, step, sections, info, a, b, edge_in, fixed, typed, free, scratch):
    rows, width = a.shape
    lead = 4 + len(fixed)
    state = (*typed, *free)
    like = jax.ShapeDtypeStruct((rows, width), BF16)
    return pl.pallas_call(
        partial(kernel, step, sections),
        out_shape=(like, *map(held, typed), *[jax.ShapeDtypeStruct(x.shape, x.dtype) for x in free]),
        in_specs=[SMEM] + [ANY] * 3 + [VMEM] * (len(fixed) + len(typed)) + [ANY] * len(free),
        out_specs=(ANY,) + (VMEM,) * len(typed) + (ANY,) * len(free),
        scratch_shapes=[pltpu.VMEM((rows, width), BF16)] * 2 + scratch
        + [pltpu.VMEM((rows, width), BF16), pltpu.SemaphoreType.DMA((8,))],
        input_output_aliases={lead + i: 1 + i for i in range(len(state))},
        compiler_params=pltpu.CompilerParams(vmem_limit_bytes=LIMIT),
        name=name,
    )(info, a, b, edge_in, *fixed, *state)


def per_device(latents, caption_kv, caption_mask, query_weight, out_weight, gate, cotangent):
    _, micro, tok, width = latents.shape
    rows = micro * tok // CHUNKS
    inner = out_weight.shape[1]
    sections = lax.axis_size("pipe")
    sides = lax.axis_size("mp")
    replicas = lax.axis_size("dp")
    pos = lax.axis_index("pipe")
    side = lax.axis_index("mp")
    share = width // sides
    start = latents.reshape(CHUNKS, rows, width)
    cot = cotangent.reshape(CHUNKS, rows, width)
    axes = ("pipe", "mp")
    info = jnp.stack([pos, side]).astype(jnp.int32)

    def spot(p, m):
        return p * sides + m

    def shift(value, sources, step, swap):
        pairs = [(spot(p, m), spot(p + step, (1 - m) if swap else m)) for p in sources for m in range(sides)]
        return lax.ppermute(value, axes, pairs)

    def swap_sides(value, p):
        return lax.ppermute(value, axes, [(spot(p, m), spot(p, 1 - m)) for m in range(sides)])

    full = ((CHUNKS, rows, width), BF16)
    mid = ((CHUNKS, rows, inner), F32)
    narrow = ((CHUNKS, rows, inner), BF16)
    part = ((CHUNKS, rows, share), BF16)
    weights = (query_weight[0], out_weight[0], caption_kv[0, 0], caption_mask, gate)
    free = [narrow, part, part, part, full, part, part, part, ((rows, width), BF16)]
    wq, wo, kv, live, gain, xs, qr, pr, *loaded = run_load(
        weights, [pltpu.VMEM(*x) for x in (full, mid, mid)], [jax.ShapeDtypeStruct(*x) for x in free]
    )
    shared, ahead, behind = [xs, qr, pr], loaded[:4], loaded[4:8]
    ahead_scratch = [pltpu.VMEM((rows, inner), BF16)]
    behind_scratch = [pltpu.VMEM((rows, width), BF16)] + [pltpu.VMEM((rows, inner), BF16)] * 2
    turns = sections + CHUNKS - 1
    a = b = c = d = loaded[8]
    for t in range(sections - 1 + turns):
        f = t
        if f < turns:
            out, *state = run_step(
                forward_kernel, "section_forward", f, sections, info, a, b, start,
                (wq, wo, kv, live, gain), shared, ahead, ahead_scratch,
            )
            shared, ahead = state[:3], state[3:]
            sources = [p for p in range(sections - 1) if 0 <= f - p < CHUNKS]
            if sources:
                a = shift(out, sources, 1, False)
                b = shift(out, sources, 1, True)
        g = t - (sections - 1)
        if 0 <= g < turns:
            if g == CHUNKS:
                attended, again = lax.optimization_barrier((ahead[0], (weights, out)))
                everyone = lax.all_gather(attended.reshape(CHUNKS * rows, inner), "dp", axis=0, tiled=True)
                wq, wo, kv, live, gain = run_load(again[0], [], [])
            out, *state = run_step(
                backward_kernel, "section_backward", g, sections, info, c, d, cot,
                (wq, wo, kv, gain), shared, behind, behind_scratch,
            )
            shared, behind = state[:3], state[3:]
            sources = [p for p in range(1, sections) if 0 <= g - (sections - 1 - p) < CHUNKS]
            if sources:
                c = shift(out, sources, -1, False)
                d = shift(out, sources, -1, True)
    _, xh, last, last_other = ahead
    dp, dyh, low, low_other = behind
    pos, _ = lax.optimization_barrier((pos, out))

    from_next = shift(xh, list(range(1, sections)), -1, False)
    last_theirs = swap_sides(last_other, sections - 1)
    from_before = shift(dyh, list(range(sections - 1)), 1, False)
    low_theirs = swap_sides(low_other, 0)

    def total(mine, theirs):
        return (mine.astype(F32) + theirs.astype(F32)).astype(BF16)

    section_out = jnp.where(pos == sections - 1, total(last, last_theirs), from_next)
    input_grad = jnp.where(pos == 0, total(low, low_theirs), from_before)

    columns = dp.reshape(CHUNKS * rows, width).T.reshape(replicas, width // replicas, CHUNKS * rows)
    columns = lax.all_to_all(columns, "dp", split_axis=0, concat_axis=0, tiled=True)
    weight_grad = jnp.einsum(
        "srk,sdr->kd", everyone.reshape(replicas, CHUNKS * rows, inner), columns, preferred_element_type=F32
    )
    return (
        section_out.reshape(1, 1, micro, tok, share),
        input_grad.reshape(1, 1, micro, tok, share),
        weight_grad[None],
    )


def solution(mesh):
    return jax.shard_map(
        per_device,
        mesh=mesh,
        in_specs=(
            P("dp", None, None, None),
            P("dp", "pipe", None, None, "mp"),
            P("dp", None),
            P("pipe", None, "mp"),
            P("pipe", "mp", None),
            P("pipe", None),
            P("dp", None, None, None),
        ),
        out_specs=(
            P("pipe", "dp", None, None, "mp"),
            P("pipe", "dp", None, None, "mp"),
            P("pipe", "mp", "dp"),
        ),
        check_vma=False,
    )
```
